32 devices in a mesh: peer: 2 (over core), dp: 4 (over y, x), vocab: 4 (over z).
Axes of the slice: x: 2, y: 2, z: 4, core: 2. Of those that a mesh axis runs over, the one named last changes fastest.
Arguments:
- hidden: bfloat16 [2, 2048, 4096], P('peer', 'dp', 'vocab'), may hold values from -400 to 400, as said below
- head_weight: bfloat16 [2, 4096, 32000], P('peer', None, 'vocab'), may hold values from -0.09375 to 0.09375
- targets: int32 [2048], P('dp'), may hold values from 0 to 31999
Outputs:
- hidden_grad: float32 [2, 2048, 4096], P('peer', 'dp', 'vocab')
The draws below stay inside these ranges and needn't reach their ends.
Inputs may be any that keep to these rules, and one draw needn't show every extreme that they name: `hidden`: finite values.
All inputs are finite; a program needn't handle non-finite values.
Results may differ from the reference program's by a relative error of at most 0.004.
Values may be sent and summed in bfloat16 or wider, within the bound.
A program may use at most 192 MiB of HBM per device.

```python
import math
import jax
import jax.numpy as jnp
import numpy as np

D = 4096
VOCAB = 32000
TOKENS = 2048
N_VOCAB = 4


def draw_hidden(key, part):
    first = jax.random.fold_in(key, 0)
    values = 3.0 * jax.random.normal(first, (2, TOKENS, D), jnp.float32)
    return jnp.clip(values, -400.0, 400.0).astype(jnp.bfloat16)


def place_ends(result, rng, least, high):
    shape = result.shape
    index_at = [jax.random.randint(jax.random.fold_in(rng, axis), (), 0, shape[axis]) for axis in range(len(shape))]
    result = result.at[tuple(index_at)].set(least)
    longest = shape.index(max(shape))
    index_at[longest] = (index_at[longest] + 1) % shape[longest]
    return result.at[tuple(index_at)].set(high)


def shard_levels(rng, extent, cuts, smallest, high):
    loudness, own = 1.0, jax.random.fold_in(rng, 6)
    for axis_at, parts in cuts:
        heights = jnp.exp(jax.random.uniform(jax.random.fold_in(own, axis_at), (parts,), jnp.float32, smallest / len(cuts), high / len(cuts)))
        loudness = loudness * jnp.repeat(heights, extent[axis_at] // parts).reshape([-1 if axis == axis_at else 1 for axis in range(len(extent))])
    return loudness


def rank_table(number_of, lean):
    loads = [(1 << 20) // math.isqrt(rank ** lean) + 1 for rank in range(1, number_of + 1)]
    width = 1 + sum(loads) // (1 << 30)
    return np.cumsum(np.array([max(1, weight // width) for weight in loads]))


def ranked_ids(stream_key, shape, count, slope):
    listing = rank_table(count, slope)
    pick = jax.random.randint(jax.random.fold_in(stream_key, 1), shape, 0, int(listing[count - 1]))
    grade = jnp.searchsorted(jnp.asarray(listing, jnp.int32), pick, side="right")
    return jax.random.permutation(jax.random.fold_in(stream_key, 2), count)[grade].astype(jnp.int32)


def normal_values(key, dims, scale, bound, cuts=(), kind=jnp.bfloat16):
    factor_of = shard_levels(key, dims, cuts, -0.22, 0.18) if cuts else 1.0
    array = jax.random.normal(key, dims, jnp.float32) * scale * factor_of
    return jnp.minimum(jnp.maximum(array, -bound), bound).astype(kind)


def setup_inputs(seed: int = 0) -> dict:
    seeds = jax.random.split(jax.random.key(seed), 4)
    hidden = draw_hidden(jax.random.fold_in(seeds[3], 71), 0)
    head_weight = normal_values(seeds[1], (2, D, VOCAB), D ** -0.5, 0.09375, ((0, 2), (2, 4)))
    targets = place_ends(ranked_ids(seeds[2], (TOKENS,), VOCAB, 2), jax.random.fold_in(seeds[2], 3), 0, VOCAB - 1).astype(jnp.int32)
    return dict(hidden=hidden, head_weight=head_weight, targets=targets)


temper = 2.0
mixing = 0.5
loss_scale = 64.0


def reference(hidden, head_weight, targets):
    column_ids = jnp.arange(VOCAB, dtype=jnp.int32)
    onehot = (targets[:, None] == column_ids[None, :]).astype(jnp.float32)
    probs_all = []
    soft_all = []
    for peer_id in range(2):
        logits = jnp.dot(hidden[peer_id], head_weight[peer_id], preferred_element_type=jnp.float32)
        top = jnp.max(logits, axis=1, keepdims=True)
        expo = jnp.exp(logits - top)
        probs_all.append(expo / jnp.sum(expo, axis=1, keepdims=True))
        cooled = logits / temper
        top_soft = jnp.max(cooled, axis=1, keepdims=True)
        expo_soft = jnp.exp(cooled - top_soft)
        soft_all.append((expo_soft / jnp.sum(expo_soft, axis=1, keepdims=True)).astype(jnp.bfloat16))
    block = VOCAB // N_VOCAB
    grads = []
    for peer_id in range(2):
        own = soft_all[peer_id].astype(jnp.float32)
        other = soft_all[1 - peer_id].astype(jnp.float32)
        logit_grad = (loss_scale * ((probs_all[peer_id] - onehot) + mixing * temper * (own - other))).astype(jnp.bfloat16)
        summed = jnp.zeros((hidden.shape[1], D), jnp.float32)
        for shard in range(N_VOCAB):
            grad_block = logit_grad[:, shard * block:(shard + 1) * block]
            weight_block = head_weight[peer_id][:, shard * block:(shard + 1) * block]
            summed = summed + jnp.dot(grad_block, weight_block.T, preferred_element_type=jnp.float32)
        grads.append(summed)
    return jnp.stack(grads, axis=0)
```

```python
import functools

import jax
import jax.numpy as jnp
from jax import lax
from jax.experimental import pallas as pl
from jax.experimental.pallas import tpu as pltpu
from jax.sharding import PartitionSpec as P

temper = 2.0
mixing = 0.5
loss_scale = 64.0

WIRE = jnp.int16
WIRE_TOP = 32766.0
PIECES = 2
LAG = 2
HALF_LOG2E = 0.7213475204444817


def from_partner(x, axis, bit):
    return lax.ppermute(x, axis, [(i, i ^ 1 << bit) for i in range(lax.axis_size(axis))])


def plain_body(hidden, head_weight, targets):
    states = hidden[0]
    weight = head_weight[0]
    local_vocab = weight.shape[1]
    gathered = lax.all_gather(states, "vocab", axis=1, tiled=True)
    logits = jnp.dot(gathered, weight, preferred_element_type=jnp.float32)
    cooled = logits / temper
    local_top = jnp.max(logits, axis=1)
    local_cool = jnp.max(cooled, axis=1)
    top, cool = lax.pmax((local_top, local_cool), "vocab")
    local_total = jnp.sum(jnp.exp(logits - top[:, None]), axis=1)
    local_cool_total = jnp.sum(jnp.exp(cooled - cool[:, None]), axis=1)
    total, cool_total = lax.psum((local_total, local_cool_total), "vocab")
    probs = jnp.exp(logits - top[:, None]) / total[:, None]
    soft = (jnp.exp(cooled - cool[:, None]) / cool_total[:, None]).astype(jnp.bfloat16)
    other_soft = from_partner(soft, "peer", 0)
    column_ids = lax.axis_index("vocab") * local_vocab + jnp.arange(local_vocab, dtype=jnp.int32)
    onehot = (targets[:, None] == column_ids[None, :]).astype(jnp.float32)
    logit_grad = (
        loss_scale
        * (
            probs
            - onehot
            + mixing * temper * (soft.astype(jnp.float32) - other_soft.astype(jnp.float32))
        )
    ).astype(jnp.bfloat16)
    shares = lax.psum_scatter(
        lax.dot_general(
            weight, logit_grad, (((1,), (1,)), ((), ())), preferred_element_type=jnp.float32
        ),
        "vocab",
        scatter_dimension=0,
        tiled=True,
    )
    return shares.T[None]


def kernel(
    n, hidden_ref, weight_ref, targets_ref, out_ref,
    held, logits, wbuf, soft, grad, wire, unit, stat, rows_buf,
    own_sem, wsem, gather_recv, right_sem, left_sem,
    stat_send, stat_recv, soft_send, soft_recv, wire_send, wire_recv, unit_send, unit_recv, out_sem,
):
    z = lax.axis_index("vocab")
    other = 1 - lax.axis_index("peer")
    tokens, vocab = logits.shape
    steps = n * PIECES
    depth = held.shape[2]

    def remote(src, dst, send, recv, **where):
        return pltpu.make_async_remote_copy(
            src_ref=src, dst_ref=dst, send_sem=send, recv_sem=recv,
            device_id=where, device_id_type=pl.DeviceIdType.MESH,
        )

    def order(j):
        both = jnp.minimum(z, n - 1 - z) * PIECES
        k = j - PIECES
        paired = k < 2 * both
        p = jnp.where(paired, lax.div(jnp.maximum(k, 0), 2), k - both)
        leftward = jnp.where(paired, lax.rem(jnp.maximum(k, 0), 2) == 0, z > n - 1 - z)
        p = jnp.maximum(p, 0)
        far = 1 + lax.div(p, PIECES)
        shard = jnp.where(j < PIECES, z, jnp.where(leftward, z - far, z + far))
        piece = jnp.where(j < PIECES, j, lax.rem(p, PIECES))
        return shard, piece, both

    def place(j):
        shard, piece, _ = order(j)
        return shard * PIECES + piece

    def load_weight(j, slot):
        row = pl.multiple_of(place(j) * depth, depth)
        return pltpu.make_async_copy(
            weight_ref.at[0, pl.ds(row, depth), :], wbuf.at[slot], wsem.at[slot]
        )

    def send_right(at):
        return remote(held.at[at], held.at[at], right_sem.at[at], gather_recv.at[at], vocab=jnp.minimum(z + 1, n - 1))

    def send_left(at):
        return remote(held.at[at], held.at[at], left_sem.at[at], gather_recv.at[at], vocab=jnp.maximum(z - 1, 0))

    load_weight(0, 0).start()
    own = [
        pltpu.make_async_copy(
            hidden_ref.at[0, :, pl.ds(c * depth, depth)], held.at[z * PIECES + c], own_sem.at[c]
        )
        for c in range(PIECES)
    ]
    for copy in own:
        copy.start()

    barrier = pltpu.get_barrier_semaphore()
    for o in range(1, n):
        pl.semaphore_signal(
            barrier, inc=1, device_id={"vocab": lax.rem(z + o, n)}, device_id_type=pl.DeviceIdType.MESH
        )
    pl.semaphore_signal(barrier, inc=1, device_id={"peer": other}, device_id_type=pl.DeviceIdType.MESH)
    pl.semaphore_wait(barrier, n)

    for c in range(PIECES):
        own[c].wait()

        @pl.when(z < n - 1)
        def _():
            send_right(z * PIECES + c).start()

        @pl.when(z > 0)
        def _():
            send_left(z * PIECES + c).start()

    block = 32

    @pl.loop(0, tokens // block)
    def _(r):
        logits[pl.ds(pl.multiple_of(r * block, block), block), :] = jnp.zeros((block, vocab), jnp.float32)

    def arrive(at, leftward):
        remote(held.at[at], held.at[at], right_sem.at[at], gather_recv.at[at], peer=other).wait_recv()

        @pl.when(jnp.logical_and(leftward, z < n - 1))
        def _():
            send_right(at).start()

        @pl.when(jnp.logical_and(jnp.logical_not(leftward), z > 0))
        def _():
            send_left(at).start()

    width = 1024
    whole = vocab // width

    @pl.loop(0, steps)
    def _(j):
        slot = lax.rem(j, 2)
        shard, piece, both = order(j)
        at = shard * PIECES + piece
        k = j - PIECES
        paired = jnp.logical_and(k >= 0, k < 2 * both)
        first = jnp.logical_and(paired, lax.rem(jnp.maximum(k, 0), 2) == 0)
        single = k >= 2 * both

        @pl.when(j + 1 < steps)
        def _():
            load_weight(j + 1, 1 - slot).start()

        @pl.when(jnp.logical_and(k >= 0, jnp.logical_or(first, single)))
        def _():
            arrive(at, shard < z)

        @pl.when(first)
        def _():
            arrive(place(j + 1), jnp.bool_(False))

        load_weight(j, slot).wait()
        x = held.at[at]
        w = wbuf.at[slot]

        @pl.loop(0, whole)
        def _(t):
            cols = pl.ds(pl.multiple_of(t * width, width), width)
            logits[:, cols] += jnp.dot(x[...], w[:, cols], preferred_element_type=jnp.float32)

        if whole * width < vocab:
            cols = pl.ds(whole * width, vocab - whole * width)
            logits[:, cols] += jnp.dot(x[...], w[:, cols], preferred_element_type=jnp.float32)

    lane = lax.broadcasted_iota(jnp.int32, (block, 128), 1)

    @pl.loop(0, tokens // block)
    def _(r):
        rows = pl.ds(pl.multiple_of(r * block, block), block)
        x = logits[rows, :]
        top = jnp.max(x, axis=1, keepdims=True)
        e = jnp.exp2((x - top) * HALF_LOG2E)
        logits[rows, :] = e
        cool = jnp.sum(e, axis=1, keepdims=True)
        total = jnp.sum(e * e, axis=1, keepdims=True)
        stat[rows, :] = jnp.where(lane == 0, top, jnp.where(lane == 1, total, cool))

    rows_buf[z] = stat[...].T[:8]

    def stat_copy(o):
        return remote(
            rows_buf.at[z], rows_buf.at[z], stat_send.at[o], stat_recv.at[z], vocab=lax.rem(z + o, n)
        )

    for o in range(1, n):
        stat_copy(o).start()
    for o in range(1, n):
        source = lax.rem(z + o, n)
        remote(rows_buf.at[source], rows_buf.at[source], stat_send.at[o], stat_recv.at[source], peer=other).wait_recv()

    top = rows_buf[0, 0:1, :]
    for i in range(1, n):
        top = jnp.maximum(top, rows_buf[i, 0:1, :])
    total = jnp.zeros_like(top)
    cool = jnp.zeros_like(top)
    for i in range(n):
        shrink = jnp.exp((rows_buf[i, 0:1, :] - top) * 0.5)
        total += rows_buf[i, 1:2, :] * (shrink * shrink)
        cool += rows_buf[i, 2:3, :] * shrink
    shrink = jnp.exp((rows_buf[z, 0:1, :] - top) * 0.5)
    hard_scale = (shrink * shrink) / total
    soft_scale = shrink / cool
    pick = lax.broadcasted_iota(jnp.int32, (128, tokens), 0)
    stat[...] = jnp.where(pick == 0, hard_scale, soft_scale).T

    group = 64
    groups = tokens // group

    def soft_copy(r):
        rows = pl.ds(pl.multiple_of(r * group, group), group)
        return remote(soft.at[rows, :], grad.at[rows, :], soft_send.at[r], soft_recv.at[r], peer=other)

    @pl.loop(0, groups)
    def _(r):
        rows = pl.ds(pl.multiple_of(r * group, group), group)
        soft[rows, :] = (logits[rows, :] * stat[rows, 1:2]).astype(jnp.bfloat16)
        soft_copy(r).start()

    sub = 32

    @pl.loop(0, groups)
    def _(r):
        soft_copy(r).wait_recv()

        @pl.loop(0, group // sub)
        def _(q):
            rows = pl.ds(pl.multiple_of(r * group + q * sub, sub), sub)
            e = logits[rows, :]
            ids = lax.broadcasted_iota(jnp.int32, (sub, vocab), 1)
            onehot = jnp.where(ids == targets_ref[rows, :] - z * vocab, 1.0, 0.0)
            gap = soft[rows, :].astype(jnp.float32) - grad[rows, :].astype(jnp.float32)
            full = (e * e) * stat[rows, 0:1] - onehot + (mixing * temper) * gap
            grad[rows, :] = (loss_scale * full).astype(jnp.bfloat16)

    features = 256

    def columns(at):
        return pl.ds(pl.multiple_of(at * depth, depth), depth)

    def wire_in(slot):
        remote(unit.at[slot], unit.at[slot], unit_send.at[0], unit_recv.at[slot], peer=other).wait_recv()
        remote(wire.at[slot], wire.at[slot], wire_send.at[0], wire_recv.at[slot], peer=other).wait_recv()

    def wire_out(at, dst, target):
        return (
            remote(unit.at[at], unit.at[dst], unit_send.at[at], unit_recv.at[dst], vocab=target),
            remote(wire.at[at], wire.at[dst], wire_send.at[at], wire_recv.at[dst], vocab=target),
        )

    def wire_start(at, dst, target):
        for copy in wire_out(at, dst, target):
            copy.start()

    def out_copy(c):
        return pltpu.make_async_copy(
            logits.at[:, columns(z * PIECES + c)], out_ref.at[0, :, pl.ds(c * depth, depth)], out_sem.at[c]
        )

    def pass_on(i):
        shard, piece, _ = order(steps - 1 - i)
        at = shard * PIECES + piece
        cols = columns(at)

        def add(slot):
            wire_in(slot)
            logits[:, cols] += wire[slot].astype(jnp.int32).astype(jnp.float32) * unit[slot, 0:1, :]

        @pl.when(jnp.logical_and(shard <= z, z < n - 1))
        def _():
            add(at)

        @pl.when(jnp.logical_and(shard >= z, z > 0))
        def _():
            add(jnp.where(shard == z, steps + piece, at))

        @pl.when(shard != z)
        def _():
            value = logits[:, cols]
            peak = jnp.maximum(jnp.max(jnp.abs(value), axis=0, keepdims=True), 1e-30)
            unit[at] = jnp.broadcast_to(peak * (1.0 / WIRE_TOP), (8, depth))
            wire[at] = jnp.round(value * (WIRE_TOP / peak)).astype(jnp.int32).astype(WIRE)

        @pl.when(shard < z)
        def _():
            wire_start(at, at, jnp.maximum(z - 1, 0))

        @pl.when(shard > z)
        def _():
            wire_start(at, jnp.where(shard == z + 1, steps + piece, at), jnp.minimum(z + 1, n - 1))

        @pl.when(shard == z)
        def _():
            out_copy(piece).start()

    @pl.loop(0, steps + LAG)
    def _(i):
        @pl.when(i < steps)
        def _():
            j = steps - 1 - i
            slot = lax.rem(j, 2)
            at = place(j)

            @pl.when(i >= 2)
            def _():
                load_weight(j, slot).wait()

            @pl.loop(0, depth // features)
            def _(t):
                w = wbuf.at[slot, pl.ds(pl.multiple_of(t * features, features), features), :]
                logits[:, pl.ds(pl.multiple_of(at * depth + t * features, features), features)] = lax.dot_general(
                    grad[...], w[...], (((1,), (1,)), ((), ())), preferred_element_type=jnp.float32
                )

            @pl.when(i + 2 < steps)
            def _():
                load_weight(j - 2, slot).start()

        @pl.when(i >= LAG)
        def _():
            pass_on(i - LAG)

    for at in range(steps):
        shard = at // PIECES

        @pl.when(jnp.logical_and(shard <= z, z < n - 1))
        def _():
            send_right(at).wait_send()

        @pl.when(jnp.logical_and(shard >= z, z > 0))
        def _():
            send_left(at).wait_send()

        @pl.when(shard != z)
        def _():
            for copy in wire_out(at, at, jnp.where(z > 0, z - 1, 1)):
                copy.wait_send()

    for o in range(1, n):
        stat_copy(o).wait_send()

    @pl.loop(0, groups)
    def _(r):
        soft_copy(r).wait_send()

    for c in range(PIECES):
        out_copy(c).wait()


def fused_body(n, hidden, head_weight, targets):
    _, tokens, own = hidden.shape
    vocab = head_weight.shape[2]
    depth = own // PIECES
    steps = n * PIECES
    dma = pltpu.SemaphoreType.DMA
    return pl.pallas_call(
        functools.partial(kernel, n),
        out_shape=jax.ShapeDtypeStruct((1, tokens, own), jnp.float32),
        in_specs=[
            pl.BlockSpec(memory_space=pl.ANY),
            pl.BlockSpec(memory_space=pl.ANY),
            pl.BlockSpec(memory_space=pltpu.VMEM),
        ],
        out_specs=pl.BlockSpec(memory_space=pl.ANY),
        scratch_shapes=[
            pltpu.VMEM((steps, tokens, depth), jnp.bfloat16),
            pltpu.VMEM((tokens, vocab), jnp.float32),
            pltpu.VMEM((2, depth, vocab), jnp.bfloat16),
            pltpu.VMEM((tokens, vocab), jnp.bfloat16),
            pltpu.VMEM((tokens, vocab), jnp.bfloat16),
            pltpu.VMEM((steps + PIECES, tokens, depth), WIRE),
            pltpu.VMEM((steps + PIECES, 8, depth), jnp.float32),
            pltpu.VMEM((tokens, 128), jnp.float32),
            pltpu.VMEM((n, 8, tokens), jnp.float32),
            dma((PIECES,)),
            dma((2,)),
            dma((steps,)),
            dma((steps,)),
            dma((steps,)),
            dma((n,)),
            dma((n,)),
            dma((tokens // 64,)),
            dma((tokens // 64,)),
            dma((steps,)),
            dma((steps + PIECES,)),
            dma((steps,)),
            dma((steps + PIECES,)),
            dma((PIECES,)),
        ],
        compiler_params=pltpu.CompilerParams(
            collective_id=0, has_side_effects=True, vmem_limit_bytes=63 << 20
        ),
    )(hidden, head_weight, targets[:, None])


def solution(mesh):
    n = mesh.shape["vocab"]

    def body(hidden, head_weight, targets):
        _, tokens, own = hidden.shape
        vocab = head_weight.shape[2]
        fits = tokens * vocab * 8 + own * vocab * 2 + tokens * own * n * 4
        if n > 4 or own % (256 * PIECES) or tokens % 128 or n * own > vocab or fits > 59 << 20:
            return plain_body(hidden, head_weight, targets)
        return fused_body(n, hidden, head_weight, targets)

    return jax.shard_map(
        body,
        mesh=mesh,
        in_specs=(P("peer", "dp", "vocab"), P("peer", None, "vocab"), P("dp")),
        out_specs=P("peer", "dp", "vocab"),
        check_vma=False,
    )
```

```python
import functools

import jax
import jax.numpy as jnp
from jax import lax
from jax.experimental import pallas as pl
from jax.experimental.pallas import tpu as pltpu
from jax.sharding import PartitionSpec as P

temper = 2.0
mixing = 0.5
loss_scale = 64.0

WIRE = jnp.int16
WIRE_TOP = 32766.0
PIECES = 2
LAG = 2
HALF_LOG2E = 0.7213475204444817


def from_partner(x, axis, bit):
    return lax.ppermute(x, axis, [(i, i ^ 1 << bit) for i in range(lax.axis_size(axis))])


def plain_body(hidden, head_weight, targets):
    states = hidden[0]
    weight = head_weight[0]
    local_vocab = weight.shape[1]
    gathered = lax.all_gather(states, "vocab", axis=1, tiled=True)
    logits = jnp.dot(gathered, weight, preferred_element_type=jnp.float32)
    cooled = logits / temper
    local_top = jnp.max(logits, axis=1)
    local_cool = jnp.max(cooled, axis=1)
    top, cool = lax.pmax((local_top, local_cool), "vocab")
    local_total = jnp.sum(jnp.exp(logits - top[:, None]), axis=1)
    local_cool_total = jnp.sum(jnp.exp(cooled - cool[:, None]), axis=1)
    total, cool_total = lax.psum((local_total, local_cool_total), "vocab")
    probs = jnp.exp(logits - top[:, None]) / total[:, None]
    soft = (jnp.exp(cooled - cool[:, None]) / cool_total[:, None]).astype(jnp.bfloat16)
    other_soft = from_partner(soft, "peer", 0)
    column_ids = lax.axis_index("vocab") * local_vocab + jnp.arange(local_vocab, dtype=jnp.int32)
    onehot = (targets[:, None] == column_ids[None, :]).astype(jnp.float32)
    logit_grad = (
        loss_scale
        * (
            probs
            - onehot
            + mixing * temper * (soft.astype(jnp.float32) - other_soft.astype(jnp.float32))
        )
    ).astype(jnp.bfloat16)
    shares = lax.psum_scatter(
        lax.dot_general(
            weight, logit_grad, (((1,), (1,)), ((), ())), preferred_element_type=jnp.float32
        ),
        "vocab",
        scatter_dimension=0,
        tiled=True,
    )
    return shares.T[None]


def kernel(
    n, hidden_ref, weight_ref, targets_ref, out_ref,
    held, logits, wbuf, soft, grad, wire, unit, stat, rows_buf,
    own_sem, wsem, gather_recv, right_sem, left_sem,
    stat_send, stat_recv, soft_send, soft_recv, wire_send, wire_recv, unit_send, unit_recv, out_sem,
):
    z = lax.axis_index("vocab")
    other = 1 - lax.axis_index("peer")
    tokens, vocab = logits.shape
    steps = n * PIECES
    depth = held.shape[2]

    def remote(src, dst, send, recv, **where):
        return pltpu.make_async_remote_copy(
            src_ref=src, dst_ref=dst, send_sem=send, recv_sem=recv,
            device_id=where, device_id_type=pl.DeviceIdType.MESH,
        )

    def order(j):
        both = jnp.minimum(z, n - 1 - z) * PIECES
        k = j - PIECES
        paired = k < 2 * both
        p = jnp.where(paired, lax.div(jnp.maximum(k, 0), 2), k - both)
        leftward = jnp.where(paired, lax.rem(jnp.maximum(k, 0), 2) == 0, z > n - 1 - z)
        p = jnp.maximum(p, 0)
        far = 1 + lax.div(p, PIECES)
        shard = jnp.where(j < PIECES, z, jnp.where(leftward, z - far, z + far))
        piece = jnp.where(j < PIECES, j, lax.rem(p, PIECES))
        return shard, piece, both

    def place(j):
        shard, piece, _ = order(j)
        return shard * PIECES + piece

    def load_weight(j, slot):
        row = pl.multiple_of(place(j) * depth, depth)
        return pltpu.make_async_copy(
            weight_ref.at[0, :, pl.ds(row, depth)], wbuf.at[slot], wsem.at[slot]
        )

    def send_right(at):
        return remote(held.at[at], held.at[at], right_sem.at[at], gather_recv.at[at], vocab=jnp.minimum(z + 1, n - 1))

    def send_left(at):
        return remote(held.at[at], held.at[at], left_sem.at[at], gather_recv.at[at], vocab=jnp.maximum(z - 1, 0))

    load_weight(0, 0).start()
    own = [
        pltpu.make_async_copy(
            hidden_ref.at[0, :, pl.ds(c * depth, depth)], held.at[z * PIECES + c], own_sem.at[c]
        )
        for c in range(PIECES)
    ]
    for copy in own:
        copy.start()

    barrier = pltpu.get_barrier_semaphore()
    for o in range(1, n):
        pl.semaphore_signal(
            barrier, inc=1, device_id={"vocab": lax.rem(z + o, n)}, device_id_type=pl.DeviceIdType.MESH
        )
    pl.semaphore_signal(barrier, inc=1, device_id={"peer": other}, device_id_type=pl.DeviceIdType.MESH)
    pl.semaphore_wait(barrier, n)

    for c in range(PIECES):
        own[c].wait()

        @pl.when(z < n - 1)
        def _():
            send_right(z * PIECES + c).start()

        @pl.when(z > 0)
        def _():
            send_left(z * PIECES + c).start()

    block = 32

    @pl.loop(0, tokens // block)
    def _(r):
        logits[pl.ds(pl.multiple_of(r * block, block), block), :] = jnp.zeros((block, vocab), jnp.float32)

    def arrive(at, leftward):
        remote(held.at[at], held.at[at], right_sem.at[at], gather_recv.at[at], peer=other).wait_recv()

        @pl.when(jnp.logical_and(leftward, z < n - 1))
        def _():
            send_right(at).start()

        @pl.when(jnp.logical_and(jnp.logical_not(leftward), z > 0))
        def _():
            send_left(at).start()

    width = 1024
    whole = vocab // width

    @pl.loop(0, steps)
    def _(j):
        slot = lax.rem(j, 2)
        shard, piece, both = order(j)
        at = shard * PIECES + piece
        k = j - PIECES
        paired = jnp.logical_and(k >= 0, k < 2 * both)
        first = jnp.logical_and(paired, lax.rem(jnp.maximum(k, 0), 2) == 0)
        single = k >= 2 * both

        @pl.when(j + 1 < steps)
        def _():
            load_weight(j + 1, 1 - slot).start()

        @pl.when(jnp.logical_and(k >= 0, jnp.logical_or(first, single)))
        def _():
            arrive(at, shard < z)

        @pl.when(first)
        def _():
            arrive(place(j + 1), jnp.bool_(False))

        load_weight(j, slot).wait()
        x = held.at[at]
        w = wbuf.at[slot]

        @pl.loop(0, whole)
        def _(t):
            cols = pl.ds(pl.multiple_of(t * width, width), width)
            logits[:, cols] += lax.dot_general(
                x[...], w[cols, :], (((1,), (1,)), ((), ())), preferred_element_type=jnp.float32
            )

        if whole * width < vocab:
            cols = pl.ds(whole * width, vocab - whole * width)
            logits[:, cols] += lax.dot_general(
                x[...], w[cols, :], (((1,), (1,)), ((), ())), preferred_element_type=jnp.float32
            )

    lane = lax.broadcasted_iota(jnp.int32, (block, 128), 1)

    @pl.loop(0, tokens // block)
    def _(r):
        rows = pl.ds(pl.multiple_of(r * block, block), block)
        x = logits[rows, :]
        top = jnp.max(x, axis=1, keepdims=True)
        e = jnp.exp2((x - top) * HALF_LOG2E)
        logits[rows, :] = e
        cool = jnp.sum(e, axis=1, keepdims=True)
        total = jnp.sum(e * e, axis=1, keepdims=True)
        stat[rows, :] = jnp.where(lane == 0, top, jnp.where(lane == 1, total, cool))

    rows_buf[z] = stat[...].T[:8]

    def stat_copy(o):
        return remote(
            rows_buf.at[z], rows_buf.at[z], stat_send.at[o], stat_recv.at[z], vocab=lax.rem(z + o, n)
        )

    for o in range(1, n):
        stat_copy(o).start()
    for o in range(1, n):
        source = lax.rem(z + o, n)
        remote(rows_buf.at[source], rows_buf.at[source], stat_send.at[o], stat_recv.at[source], peer=other).wait_recv()

    top = rows_buf[0, 0:1, :]
    for i in range(1, n):
        top = jnp.maximum(top, rows_buf[i, 0:1, :])
    total = jnp.zeros_like(top)
    cool = jnp.zeros_like(top)
    for i in range(n):
        shrink = jnp.exp((rows_buf[i, 0:1, :] - top) * 0.5)
        total += rows_buf[i, 1:2, :] * (shrink * shrink)
        cool += rows_buf[i, 2:3, :] * shrink
    shrink = jnp.exp((rows_buf[z, 0:1, :] - top) * 0.5)
    hard_scale = (shrink * shrink) / total
    soft_scale = shrink / cool
    pick = lax.broadcasted_iota(jnp.int32, (128, tokens), 0)
    local_target = (targets_ref[...] - z * vocab).astype(jnp.float32)
    stat[...] = jnp.where(pick == 0, hard_scale, jnp.where(pick == 1, soft_scale, local_target)).T

    group = 64
    groups = tokens // group

    def soft_copy(r):
        rows = pl.ds(pl.multiple_of(r * group, group), group)
        return remote(soft.at[rows, :], grad.at[rows, :], soft_send.at[r], soft_recv.at[r], peer=other)

    @pl.loop(0, groups)
    def _(r):
        rows = pl.ds(pl.multiple_of(r * group, group), group)
        soft[rows, :] = (logits[rows, :] * stat[rows, 1:2]).astype(jnp.bfloat16)
        soft_copy(r).start()

    sub = 32

    @pl.loop(0, groups)
    def _(r):
        soft_copy(r).wait_recv()

        @pl.loop(0, group // sub)
        def _(q):
            rows = pl.ds(pl.multiple_of(r * group + q * sub, sub), sub)
            e = logits[rows, :]
            ids = lax.broadcasted_iota(jnp.int32, (sub, vocab), 1)
            onehot = jnp.where(ids == stat[rows, 2:3].astype(jnp.int32), 1.0, 0.0)
            gap = soft[rows, :].astype(jnp.float32) - grad[rows, :].astype(jnp.float32)
            full = (e * e) * stat[rows, 0:1] - onehot + (mixing * temper) * gap
            grad[rows, :] = (loss_scale * full).astype(jnp.bfloat16)

    features = 256

    def columns(at):
        return pl.ds(pl.multiple_of(at * depth, depth), depth)

    def wire_in(slot):
        remote(unit.at[slot], unit.at[slot], unit_send.at[0], unit_recv.at[slot], peer=other).wait_recv()
        remote(wire.at[slot], wire.at[slot], wire_send.at[0], wire_recv.at[slot], peer=other).wait_recv()

    def wire_out(at, dst, target):
        return (
            remote(unit.at[at], unit.at[dst], unit_send.at[at], unit_recv.at[dst], vocab=target),
            remote(wire.at[at], wire.at[dst], wire_send.at[at], wire_recv.at[dst], vocab=target),
        )

    def wire_start(at, dst, target):
        for copy in wire_out(at, dst, target):
            copy.start()

    def out_copy(c):
        return pltpu.make_async_copy(
            logits.at[:, columns(z * PIECES + c)], out_ref.at[0, :, pl.ds(c * depth, depth)], out_sem.at[c]
        )

    def pass_on(i):
        shard, piece, _ = order(steps - 1 - i)
        at = shard * PIECES + piece
        cols = columns(at)

        def add(slot):
            wire_in(slot)
            logits[:, cols] += wire[slot].astype(jnp.int32).astype(jnp.float32) * unit[slot, 0:1, :]

        @pl.when(jnp.logical_and(shard <= z, z < n - 1))
        def _():
            add(at)

        @pl.when(jnp.logical_and(shard >= z, z > 0))
        def _():
            add(jnp.where(shard == z, steps + piece, at))

        @pl.when(shard != z)
        def _():
            value = logits[:, cols]
            peak = jnp.maximum(jnp.max(jnp.abs(value), axis=0, keepdims=True), 1e-30)
            unit[at] = jnp.broadcast_to(peak * (1.0 / WIRE_TOP), (8, depth))
            wire[at] = jnp.round(value * (WIRE_TOP / peak)).astype(jnp.int32).astype(WIRE)

        @pl.when(shard < z)
        def _():
            wire_start(at, at, jnp.maximum(z - 1, 0))

        @pl.when(shard > z)
        def _():
            wire_start(at, jnp.where(shard == z + 1, steps + piece, at), jnp.minimum(z + 1, n - 1))

        @pl.when(shard == z)
        def _():
            out_copy(piece).start()

    @pl.loop(0, steps + LAG)
    def _(i):
        @pl.when(i < steps)
        def _():
            j = steps - 1 - i
            slot = lax.rem(j, 2)
            at = place(j)

            @pl.when(i >= 2)
            def _():
                load_weight(j, slot).wait()

            @pl.loop(0, depth // features)
            def _(t):
                w = wbuf[slot, :, pl.ds(pl.multiple_of(t * features, features), features)]
                logits[:, pl.ds(pl.multiple_of(at * depth + t * features, features), features)] = jnp.dot(
                    grad[...], w, preferred_element_type=jnp.float32
                )

            @pl.when(i + 2 < steps)
            def _():
                load_weight(j - 2, slot).start()

        @pl.when(i >= LAG)
        def _():
            pass_on(i - LAG)

    for at in range(steps):
        shard = at // PIECES

        @pl.when(jnp.logical_and(shard <= z, z < n - 1))
        def _():
            send_right(at).wait_send()

        @pl.when(jnp.logical_and(shard >= z, z > 0))
        def _():
            send_left(at).wait_send()

        @pl.when(shard != z)
        def _():
            for copy in wire_out(at, at, jnp.where(z > 0, z - 1, 1)):
                copy.wait_send()

    for o in range(1, n):
        stat_copy(o).wait_send()

    @pl.loop(0, groups)
    def _(r):
        soft_copy(r).wait_send()

    for c in range(PIECES):
        out_copy(c).wait()


def fused_body(n, hidden, head_weight, targets):
    _, tokens, own = hidden.shape
    vocab = head_weight.shape[2]
    depth = own // PIECES
    steps = n * PIECES
    dma = pltpu.SemaphoreType.DMA
    return pl.pallas_call(
        functools.partial(kernel, n),
        out_shape=jax.ShapeDtypeStruct((1, tokens, own), jnp.float32),
        in_specs=[
            pl.BlockSpec(memory_space=pl.ANY),
            pl.BlockSpec(memory_space=pl.ANY),
            pl.BlockSpec(memory_space=pltpu.VMEM),
        ],
        out_specs=pl.BlockSpec(memory_space=pl.ANY),
        scratch_shapes=[
            pltpu.VMEM((steps, tokens, depth), jnp.bfloat16),
            pltpu.VMEM((tokens, vocab), jnp.float32),
            pltpu.VMEM((2, vocab, depth), jnp.bfloat16),
            pltpu.VMEM((tokens, vocab), jnp.bfloat16),
            pltpu.VMEM((tokens, vocab), jnp.bfloat16),
            pltpu.VMEM((steps + PIECES, tokens, depth), WIRE),
            pltpu.VMEM((steps + PIECES, 8, depth), jnp.float32),
            pltpu.VMEM((tokens, 128), jnp.float32),
            pltpu.VMEM((n, 8, tokens), jnp.float32),
            dma((PIECES,)),
            dma((2,)),
            dma((steps,)),
            dma((steps,)),
            dma((steps,)),
            dma((n,)),
            dma((n,)),
            dma((tokens // 64,)),
            dma((tokens // 64,)),
            dma((steps,)),
            dma((steps + PIECES,)),
            dma((steps,)),
            dma((steps + PIECES,)),
            dma((PIECES,)),
        ],
        compiler_params=pltpu.CompilerParams(
            collective_id=0, has_side_effects=True, vmem_limit_bytes=63 << 20
        ),
    )(hidden, jnp.swapaxes(head_weight, 1, 2), targets[None, :])


def solution(mesh):
    n = mesh.shape["vocab"]

    def body(hidden, head_weight, targets):
        _, tokens, own = hidden.shape
        vocab = head_weight.shape[2]
        fits = tokens * vocab * 8 + own * vocab * 2 + tokens * own * n * 4
        if n > 4 or own % (256 * PIECES) or tokens % 128 or n * own > vocab or fits > 59 << 20:
            return plain_body(hidden, head_weight, targets)
        return fused_body(n, hidden, head_weight, targets)

    return jax.shard_map(
        body,
        mesh=mesh,
        in_specs=(P("peer", "dp", "vocab"), P("peer", None, "vocab"), P("dp")),
        out_specs=P("peer", "dp", "vocab"),
        check_vma=False,
    )
```
